256 devices in a mesh: loop: 32 (over z, x_hi, core), grp: 8 (over y, x_lo).
Axes of the slice: x: 4 (x_hi: 2, x_lo: 2; x = x_hi * 2 + x_lo), y: 4, z: 8, core: 2. Of those that a mesh axis runs over, the one named last changes fastest.
Arguments:
- node_feats: bfloat16 [512, 65536], P(None, ('loop', 'grp')), may hold values from -6 to 6
- tile_vals: bfloat16 [32, 32, 10, 128, 128], P('loop'), may hold values from -0.375 to 0.375
- tile_rows: int32 [32, 32, 10], P('loop'), may hold values from 0 to 15
- tile_cols: int32 [32, 32, 10], P('loop'), may hold values from 0 to 15
- tile_count: int32 [32, 32], P('loop'), may hold values from 0 to 10, as said below
- degree: int32 [65536], P('loop'), may hold values from 1 to 8
- w_self: bfloat16 [512, 512], replicated, may hold values from -0.25 to 0.25
- w_neigh: bfloat16 [512, 512], replicated, may hold values from -0.25 to 0.25
Outputs:
- node_out: bfloat16 [512, 65536], P(None, ('loop', 'grp'))
The draws below stay inside these ranges and needn't reach their ends.
Inputs may be any that keep to these rules, and one draw needn't show every extreme that they name: Only the first tile_count[j, t] slots of a pair are tiles of the graph; later slots hold values that belong to no edge. Some pair uses all 10 slots in every draw.
All inputs are finite; a program needn't handle non-finite values.
Results may differ from the reference program's by a relative error of at most 0.0035.
Values may be sent and summed in bfloat16 or wider, within the bound.
No kernel may reach another device: no remote copies, remote signals or barrier semaphores. Data moves between devices by JAX's collectives and lax.ppermute only.
A program may use at most 64 MiB of HBM per device.

```python
import jax
import jax.numpy as jnp
from jax import lax

F = 512
TB = 128
CAP = 10
SET = 2048
BLOCKS = 16
NODES = 65536
N_LOOP = 32


def draw_tile_count(key, part):
    sample_one = jax.random.randint(jax.random.fold_in(key, 11), (N_LOOP, N_LOOP), 0, CAP + 1)
    sample_two = jax.random.randint(jax.random.fold_in(key, 12), (N_LOOP, N_LOOP), 0, CAP + 1)
    counts = jnp.maximum(sample_one, sample_two)
    source_pick = jax.random.randint(jax.random.fold_in(key, 13), (), 0, N_LOOP)
    target_pick = jax.random.randint(jax.random.fold_in(key, 14), (), 0, N_LOOP)
    counts = counts.at[source_pick, target_pick].set(CAP)
    return counts.astype(jnp.int32)


def plant(array, stream_key, low, top_value):
    longest = array.shape.index(max(array.shape))
    spots = []
    for shift in (0, 1):
        where = [jax.random.randint(jax.random.fold_in(stream_key, axis), (), 0, length) for axis, length in enumerate(array.shape)]
        where[longest] = (where[longest] + shift) % array.shape[longest]
        spots.append(tuple(where))
    return array.at[spots[0]].set(low).at[spots[1]].set(top_value)


def shard_levels(stream_key, shape, shards, low, top_value):
    loudness, own = 1.0, jax.random.fold_in(stream_key, 6)
    for axis_at, blocks in shards:
        draws = jnp.exp(jax.random.uniform(jax.random.fold_in(own, axis_at), (blocks,), jnp.float32, low / len(shards), top_value / len(shards)))
        loudness = loudness * jnp.repeat(draws, shape[axis_at] // blocks).reshape([-1 if axis == axis_at else 1 for axis in range(len(shape))])
    return loudness


def scatter_about(stream_key, extent, scale, reach, cuts=(), held_as=jnp.bfloat16):
    array = jax.random.normal(stream_key, extent, jnp.float32) * scale
    if len(cuts) > 0:
        array = shard_levels(stream_key, extent, cuts, -0.22, 0.18) * array
    return jnp.clip(array, min=-reach, max=reach).astype(held_as)


def setup_inputs(seed: int = 0) -> dict:
    seeds = jax.random.split(jax.random.key(seed), 9)
    return {
        "node_feats": scatter_about(seeds[0], (F, NODES), 1.0, 6.0, ((1, 256),)),
        "tile_vals": scatter_about(seeds[1], (N_LOOP, N_LOOP, CAP, TB, TB), (2 * TB) ** -0.5, 0.375, ((0, 32),)),
        "tile_rows": plant(jax.random.randint(seeds[2], (N_LOOP, N_LOOP, CAP), 0, BLOCKS), jax.random.fold_in(seeds[2], 1), 0, BLOCKS - 1).astype(jnp.int32),
        "tile_cols": plant(jax.random.randint(seeds[3], (N_LOOP, N_LOOP, CAP), 0, BLOCKS), jax.random.fold_in(seeds[3], 1), 0, BLOCKS - 1).astype(jnp.int32),
        "tile_count": draw_tile_count(jax.random.fold_in(seeds[8], 71), 0),
        "degree": plant(jax.random.randint(seeds[5], (NODES,), 1, 9), jax.random.fold_in(seeds[5], 1), 1, 8).astype(jnp.int32),
        "w_self": scatter_about(seeds[6], (F, F), F ** -0.5, 0.25),
        "w_neigh": scatter_about(seeds[7], (F, F), F ** -0.5, 0.25),
    }


def contribute(sources, tiles, row_ids, col_ids, filled):
    grouped = sources.reshape(F, BLOCKS, TB)
    chosen = jnp.take(grouped, col_ids, axis=1)
    products = jnp.einsum('fkc,krc->kfr', chosen.astype(jnp.float32), tiles.astype(jnp.float32))
    active = jnp.arange(CAP, dtype=jnp.int32) < filled
    placer = ((row_ids[:, None] == jnp.arange(BLOCKS, dtype=jnp.int32)[None, :]) & active[:, None]).astype(jnp.float32)
    spread = jnp.einsum('kb,kfr->fbr', placer, products, precision=lax.Precision.HIGHEST)
    return spread.reshape(F, SET)

def reference(node_feats, tile_vals, tile_rows, tile_cols, tile_count, degree, w_self, w_neigh):

    def for_target(target):

        def accumulate(running, source):
            sources = lax.dynamic_slice_in_dim(node_feats, (source * SET).astype(jnp.int32), SET, 1)
            added = contribute(sources, tile_vals[source, target], tile_rows[source, target], tile_cols[source, target], tile_count[source, target])
            return (running + added, None)
        running, _ = lax.scan(accumulate, jnp.zeros((F, SET), jnp.float32), jnp.arange(N_LOOP, dtype=jnp.int32))
        return running
    per_set = lax.map(for_target, jnp.arange(N_LOOP, dtype=jnp.int32))
    summed = jnp.transpose(per_set, (1, 0, 2)).reshape(F, NODES)
    neigh = (summed / degree.astype(jnp.float32)[None, :]).astype(jnp.bfloat16)
    pre = jnp.dot(w_self.T, node_feats, preferred_element_type=jnp.float32) + jnp.dot(w_neigh.T, neigh, preferred_element_type=jnp.float32)
    hidden = jnp.maximum(pre, 0.0)
    mean_square = lax.optimization_barrier(jnp.mean(hidden * hidden, axis=0, keepdims=True))
    return (hidden * lax.rsqrt(mean_square + 1e-05)).astype(jnp.bfloat16)
```

```python
import jax
import jax.numpy as jnp
from jax import lax
from jax.experimental import pallas as pl
from jax.experimental.pallas import tpu as pltpu
from jax.sharding import Mesh
from jax.sharding import PartitionSpec as P

RINGS = 8
SIDES = 2
CORES = 2
VMEM = 10 * 1024 * 1024


def tile_kernel(targets, codes, columns, tiles, *rest):
    partner, out = rest if len(rest) == 2 else (None, rest[0])
    blocks, channels, edge = out.shape[1:]
    slots = tiles.shape[1]
    target = targets[pl.program_id(0)]
    acc = out.at[0]
    acc[...] = jnp.zeros_like(acc) if partner is None else partner[0]
    per = columns.shape[2] // edge
    for slot in range(slots):
        code = codes[target * slots + slot]
        row, col = code // blocks, code % blocks
        lanes = pl.ds(pl.multiple_of((col % per) * edge, edge), edge)

        @pl.when(row < blocks)
        def _():
            chosen = columns[col // per, :, lanes]
            acc[row] += lax.dot_general(
                chosen, tiles[0, slot], (((1,), (1,)), ((), ())), preferred_element_type=jnp.float32
            )


def tile_sums(targets, codes, columns, tiles, partner=None):
    count = targets.shape[0]
    slots, edge = tiles.shape[1], tiles.shape[2]
    channels = columns.shape[1]
    blocks = columns.shape[0] * columns.shape[2] // edge
    dense = pl.BlockSpec((1, blocks, channels, edge), lambda i, *_: (i, 0, 0, 0))
    in_specs = [
        pl.BlockSpec(columns.shape, lambda i, *_: (0, 0, 0)),
        pl.BlockSpec((1, slots, edge, edge), lambda i, t, c: (t[i], 0, 0, 0)),
    ]
    operands = [columns, tiles]
    if partner is not None:
        in_specs.append(dense)
        operands.append(partner)
    return pl.pallas_call(
        tile_kernel,
        grid_spec=pltpu.PrefetchScalarGridSpec(
            num_scalar_prefetch=2, grid=(count,), in_specs=in_specs, out_specs=dense
        ),
        out_shape=jax.ShapeDtypeStruct((count, blocks, channels, edge), jnp.float32),
        compiler_params=pltpu.CompilerParams(vmem_limit_bytes=VMEM),
        cost_estimate=pl.CostEstimate(
            flops=count * 1_500_000_000, bytes_accessed=count * 800_000, transcendentals=0
        ),
    )(targets, codes, *operands)


def finish_kernel(base, neighbors, weight, out):
    size = neighbors.shape[0] * neighbors.shape[2]
    edge = neighbors.shape[3]
    for half in range(neighbors.shape[1]):
        features = neighbors[:, half].reshape(size, edge)
        lanes = slice(half * edge, (half + 1) * edge)
        combined = base[:, lanes] + lax.dot_general(
            weight[...], features, (((0,), (0,)), ((), ())), preferred_element_type=jnp.float32
        )
        hidden = jnp.maximum(combined, 0.0)
        mean_square = jnp.mean(hidden * hidden, axis=0, keepdims=True)
        out[:, lanes] = (hidden * lax.rsqrt(mean_square + 1e-05)).astype(out.dtype)


def finish(base, neighbors, weight):
    return pl.pallas_call(
        finish_kernel,
        out_shape=jax.ShapeDtypeStruct(base.shape, jnp.bfloat16),
        compiler_params=pltpu.CompilerParams(vmem_limit_bytes=VMEM),
    )(base, neighbors, weight)


def hop(values, by):
    return lax.ppermute(values, "ring", [(i, (i + by) % RINGS) for i in range(RINGS)])


def swap(values, axis):
    return lax.ppermute(values, axis, [(0, 1), (1, 0)])


def shards(node_feats, tile_vals, tile_rows, tile_cols, tile_count, degree, w_self, w_neigh):
    groups = lax.axis_size("grp")
    features, width = node_feats.shape
    ring = lax.axis_index("ring")
    side = lax.axis_index("side")
    core = lax.axis_index("core")
    columns = lax.all_to_all(
        node_feats.reshape(groups, features // groups, width), "grp", split_axis=0, concat_axis=0
    )
    tiles = tile_vals[0]
    targets_count, slots, edge = tiles.shape[:3]
    blocks = groups * width // edge
    active = lax.broadcasted_iota(jnp.int32, (targets_count, slots), 1) < tile_count[0][:, None]
    codes = (jnp.where(active, tile_rows[0], blocks) * blocks + tile_cols[0]).reshape(-1)

    def indices(steps, core_index):
        position = [((ring + by + RINGS) % RINGS * SIDES + side_index) * CORES + core_index for by, side_index in steps]
        return jnp.stack(position).astype(jnp.int32)

    mine, other = side, 1 - side
    plan = [
        [(4, mine), (-4, other)],
        [(3, mine), (3, other), (-3, mine), (-3, other)],
        [(2, mine), (2, other), (-2, mine), (-2, other)],
        [(1, mine), (1, other), (-1, mine), (-1, other)],
        [(0, mine), (0, other)],
    ]
    local = []
    for steps in plan:
        foreign = tile_sums(indices(steps, 1 - core), codes, columns, tiles)
        partner = swap(foreign, "core")
        local.append(tile_sums(indices(steps, core), codes, columns, tiles, partner))

    def low(values):
        return values.astype(jnp.bfloat16)

    up = hop(low(local[0][:1]), 1).astype(jnp.float32)
    down = hop(low(local[0][1:]), -1).astype(jnp.float32)
    here = local[1]
    send_up = jnp.stack([low(here[0] + up[0]), low(here[1])])
    send_down = jnp.stack([low(here[2]), low(here[3] + down[0])])
    for here in local[2:4]:
        up = hop(send_up, 1).astype(jnp.float32)
        down = hop(send_down, -1).astype(jnp.float32)
        send_up = low(here[:2] + up)
        send_down = low(here[2:] + down)
    up = hop(send_up, 1).astype(jnp.float32)
    down = hop(send_down, -1).astype(jnp.float32)
    own = local[4] + up + down
    summed = own[0] + swap(low(own[1]), "side").astype(jnp.float32)
    neighbor = low(summed / degree.astype(jnp.float32).reshape(blocks, 1, edge))
    neighbor = neighbor.reshape(groups, blocks // groups, features // groups, edge)
    gathered = lax.all_to_all(neighbor, "grp", split_axis=0, concat_axis=0)
    base = lax.dot_general(
        w_self, node_feats, (((0,), (0,)), ((), ())), preferred_element_type=jnp.float32
    )
    return finish(base, gathered, w_neigh)


def solution(mesh):
    fine = Mesh(
        mesh.devices.reshape(RINGS, SIDES, CORES, mesh.shape["grp"]), ("ring", "side", "core", "grp")
    )
    loop = ("ring", "side", "core")
    return jax.shard_map(
        shards,
        mesh=fine,
        in_specs=(
            P(None, (*loop, "grp")),
            P(loop, None, None, None, None),
            P(loop, None, None),
            P(loop, None, None),
            P(loop, None),
            P(loop),
            P(),
            P(),
        ),
        out_specs=P(None, (*loop, "grp")),
        check_vma=False,
    )
```

```python
import functools

import jax
import jax.numpy as jnp
from jax import lax
from jax.experimental import pallas as pl
from jax.experimental.pallas import tpu as pltpu
from jax.sharding import Mesh
from jax.sharding import PartitionSpec as P


RINGS = 8
SIDES = 2
CORES = 2
REACH = RINGS // 2
BLOCKS = 16
NEAR = 10
VMEM = 3 * 1024 * 1024
RESIDENT = pl.BlockSpec(memory_space=pltpu.VMEM)
SCALARS = pl.BlockSpec(memory_space=pltpu.SMEM)


def cores_at(distance):
    return 1 if distance in (0, REACH) else CORES


def small_call(body, operands, outs):
    return pl.pallas_call(
        body,
        in_specs=[RESIDENT] * len(operands),
        out_specs=[RESIDENT] * len(outs),
        out_shape=outs,
        compiler_params=pltpu.CompilerParams(vmem_limit_bytes=VMEM),
        cost_estimate=pl.CostEstimate(flops=500_000_000, bytes_accessed=1_000_000, transcendentals=0),
    )(*operands)


def target_of(distance, core_turn, side_turn, given):
    mine = lax.axis_index("core")
    by = jnp.where(mine == given, distance, RINGS - distance)
    ring = lax.rem(lax.axis_index("ring") + by, RINGS)
    side = lax.axis_index("side") ^ side_turn
    core = mine ^ given ^ core_turn
    return (ring * SIDES + side) * CORES + core


def add_tiles(total, target, codes, columns, tiles):
    slots, edge = tiles.shape[:2]
    blocks = total.shape[0]
    shift = blocks.bit_length() - 1
    per = columns.shape[2] // edge
    for slot in range(slots):
        code = codes[slot, target]
        row, col = code >> shift, code & (blocks - 1)
        lanes = pl.ds(pl.multiple_of((col & (per - 1)) * edge, edge), edge)
        chosen = columns[col >> (per.bit_length() - 1), :, lanes]
        chosen = jnp.where(row < blocks, chosen, jnp.zeros_like(chosen))
        total[row & (blocks - 1)] += lax.dot_general(
            chosen, tiles[slot], (((1,), (1,)), ((), ())), preferred_element_type=jnp.float32
        )


def copies_of(plan, source, out, done):
    copies = []
    for distance, given in plan:
        for core in range(cores_at(distance)):
            for side in range(SIDES):
                place = len(copies)
                target = target_of(distance, core, side, given)
                copies.append(pltpu.make_async_copy(source.at[target], out.at[place], done.at[place]))
    return copies


def places_of(plan):
    return sum(cores_at(distance) * SIDES for distance, _ in plan)


def tile_kernel(keep, give, first, ahead, codes, columns, tiles, *rest):
    copies = []
    if ahead:
        source, *rest, done = rest
        *rest, out, total = rest
        copies = copies_of(ahead, source, out, done)
    else:
        *rest, total = rest
    for copy in copies:
        copy.start()

    def add(distance, core, side, given):
        target = target_of(distance, core, side, given)
        place = target if first is None else first + core * SIDES + side
        add_tiles(total, target, codes, columns, tiles.at[place])

    if keep is not None:
        partner, late, near, cross = rest[:4]
        rest = rest[4:]

        @pl.loop(0, cores_at(keep))
        def _(core):
            for side in range(SIDES):
                index = core * SIDES + side
                total[...] = partner[index].astype(jnp.float32)
                add(keep, core, side, 0)
                late[index] = total[NEAR:].astype(late.dtype)
                out = near if side == 0 else cross
                out[core] = total[:NEAR].astype(out.dtype)

    if give is not None:
        given = rest[0]

        @pl.loop(0, cores_at(give))
        def _(core):
            for side in range(SIDES):
                total[...] = jnp.zeros_like(total)
                add(give, core, side, 1)
                given[core * SIDES + side] = total[...].astype(given.dtype)

    for copy in copies:
        copy.wait()


def tile_sums(keep, give, first, codes, columns, tiles, partner=None, ahead=(), source=None):
    edge = tiles.shape[2]
    groups, channels, width = columns.shape
    blocks = groups * width // edge
    outs = []
    work = 0
    if keep is not None:
        cores = cores_at(keep)
        work += cores * SIDES
        late = jnp.bfloat16 if keep == REACH else jnp.float32
        outs += [
            jax.ShapeDtypeStruct((cores * SIDES, blocks - NEAR, channels, edge), late),
            jax.ShapeDtypeStruct((cores, NEAR, channels, edge), jnp.float32),
            jax.ShapeDtypeStruct((cores, NEAR, channels, edge), jnp.bfloat16),
        ]
    if give is not None:
        cores = cores_at(give)
        work += cores * SIDES
        outs.append(jax.ShapeDtypeStruct((cores * SIDES, blocks, channels, edge), jnp.bfloat16))
    operands, specs = [columns, tiles], [RESIDENT, RESIDENT]
    scratch = [pltpu.VMEM((blocks, channels, edge), jnp.float32)]
    if ahead:
        operands.append(pltpu.with_memory_space_constraint(source, pltpu.HBM))
        specs.append(pl.BlockSpec(memory_space=pltpu.HBM))
        outs.append(jax.ShapeDtypeStruct((places_of(ahead), *source.shape[1:]), source.dtype))
        scratch.append(pltpu.SemaphoreType.DMA((places_of(ahead),)))
    if partner is not None:
        operands.append(partner)
        specs.append(RESIDENT)
    return pl.pallas_call(
        functools.partial(tile_kernel, keep, give, first, ahead),
        in_specs=[SCALARS] + specs,
        out_specs=[RESIDENT] * len(outs),
        out_shape=outs,
        scratch_shapes=scratch,
        compiler_params=pltpu.CompilerParams(vmem_limit_bytes=VMEM),
        cost_estimate=pl.CostEstimate(
            flops=work * 500_000_000, bytes_accessed=work * 800_000, transcendentals=0
        ),
    )(codes, *operands)


def load_kernel(plan, source, out, done):
    copies = copies_of(plan, source, out, done)
    for copy in copies:
        copy.start()
    for copy in copies:
        copy.wait()


def load(plan, tiles):
    count = places_of(plan)
    return pl.pallas_call(
        functools.partial(load_kernel, plan),
        in_specs=[pl.BlockSpec(memory_space=pltpu.HBM)],
        out_specs=RESIDENT,
        out_shape=jax.ShapeDtypeStruct((count, *tiles.shape[1:]), tiles.dtype),
        scratch_shapes=[pltpu.SemaphoreType.DMA((count,))],
        compiler_params=pltpu.CompilerParams(vmem_limit_bytes=256 * 1024),
        cost_estimate=pl.CostEstimate(flops=2_000_000_000, bytes_accessed=5_000_000, transcendentals=0),
    )(pltpu.with_memory_space_constraint(tiles, pltpu.HBM))


def sum_kernel(has_late, has_near, arrived_late, arrived_near, *refs):
    refs = list(refs)
    arrived = refs.pop(0) if arrived_late or arrived_near else None
    here = refs.pop(0) if has_late else None
    near, crossed = (refs.pop(0), refs.pop(0)) if has_near else (None, None)
    send = refs.pop(0)
    place = 0
    if has_late:
        count, depth = here.shape[:2]
        for index in range(count):
            total = here[index]
            if index < arrived_late:
                total = total + arrived[pl.ds(index * depth, depth)].astype(jnp.float32)
            send[pl.ds(place, depth)] = total.astype(send.dtype)
            place += depth
    if has_near:
        count, depth = near.shape[:2]
        start = arrived_late * (near_gap(near))
        for index in range(count):
            total = near[index] + crossed[index].astype(jnp.float32)
            if index < arrived_near:
                total = total + arrived[pl.ds(start + index * depth, depth)].astype(jnp.float32)
            send[pl.ds(place, depth)] = total.astype(send.dtype)
            place += depth
    if refs:
        depth = near_gap(near)
        moved = refs[0]
        moved[...] = arrived[pl.ds(moved.shape[0], moved.shape[0])]


def near_gap(near):
    return BLOCKS - near.shape[1]


def sums(here, near, crossed, arrived, arrived_late, arrived_near, moved=False):
    operands, blocks = [], 0
    if arrived is not None:
        operands.append(arrived)
    if here is not None:
        operands.append(here)
        blocks += here.shape[0] * here.shape[1]
    if near is not None:
        operands += [near, crossed]
        blocks += near.shape[0] * near.shape[1]
    tail = operands[-1].shape[2:]
    outs = [jax.ShapeDtypeStruct((blocks, *tail), jnp.bfloat16)]
    if moved:
        outs.append(jax.ShapeDtypeStruct((SIDES * near_gap(near), *tail), jnp.bfloat16))
    body = functools.partial(sum_kernel, here is not None, near is not None, arrived_late, arrived_near)
    return small_call(body, operands, outs)


def half_kernel(arrived, out):
    out[...] = arrived[pl.ds(out.shape[0], out.shape[0])]


def second_half(arrived):
    out = jax.ShapeDtypeStruct((arrived.shape[0] // 2, *arrived.shape[1:]), arrived.dtype)
    return small_call(half_kernel, (arrived,), [out])[0]


def across_kernel(here, arrived, moved, send):
    depth = here.shape[1]
    part = pl.ds(depth, depth)
    total = here[1] + arrived[part].astype(jnp.float32) + moved[part].astype(jnp.float32)
    send[...] = total.astype(send.dtype)


def across(here, arrived, moved):
    out = jax.ShapeDtypeStruct(here.shape[1:], jnp.bfloat16)
    return small_call(across_kernel, (here, arrived, moved), [out])[0]


def divide_kernel(near, near_cross, near_same, near_moved, late, late_cross, late_same, late_moved, degree, out):
    for block in range(degree.shape[0]):
        here, cross, same, moved, place = near, near_cross.at[0], near_same, near_moved, block
        if block >= NEAR:
            here, cross, same, moved, place = late, late_cross, late_same, late_moved, block - NEAR
        total = here[0, place] + cross[place].astype(jnp.float32)
        total = total + same[place].astype(jnp.float32) + moved[place].astype(jnp.float32)
        total = total / degree[block : block + 1].astype(jnp.float32)
        out[block // out.shape[1], block % out.shape[1]] = total.astype(out.dtype)


def divide(groups, operands):
    degree = operands[-1]
    blocks, edge = degree.shape
    out = jax.ShapeDtypeStruct((groups, blocks // groups, operands[0].shape[2], edge), jnp.bfloat16)
    return small_call(divide_kernel, operands, [out])[0]


def finish_kernel(base, weight, neighbors, out):
    edge = neighbors.shape[3]
    for part in range(neighbors.shape[1]):
        lanes = slice(part * edge, (part + 1) * edge)
        combined = base[:, lanes] + lax.dot_general(
            weight[...],
            neighbors[:, part].reshape(-1, edge),
            (((0,), (0,)), ((), ())),
            preferred_element_type=jnp.float32,
        )
        hidden = jnp.maximum(combined, 0.0)
        mean_square = jnp.mean(hidden * hidden, axis=0, keepdims=True)
        out[:, lanes] = (hidden * lax.rsqrt(mean_square + 1e-05)).astype(out.dtype)


def finish(base, weight, neighbors):
    return pl.pallas_call(
        finish_kernel,
        out_shape=jax.ShapeDtypeStruct(base.shape, jnp.bfloat16),
        compiler_params=pltpu.CompilerParams(vmem_limit_bytes=10 * 1024 * 1024),
    )(base, weight, neighbors)


def hop(values):
    pairs = []
    for ring in range(RINGS):
        for core in range(CORES):
            pairs.append((ring * CORES + core, (ring + 1 - 2 * core) % RINGS * CORES + core))
    return lax.ppermute(values, ("ring", "core"), pairs)


def swap(values, axis):
    return lax.ppermute(values, axis, [(0, 1), (1, 0)])


def shards(node_feats, tile_vals, tile_rows, tile_cols, tile_count, degree, w_self, w_neigh):
    groups = lax.axis_size("grp")
    features, width = node_feats.shape
    columns = lax.all_to_all(node_feats.reshape(groups, features // groups, width), "grp", split_axis=0, concat_axis=0)
    tiles = tile_vals[0]
    targets, slots, edge = tiles.shape[:3]
    blocks = groups * width // edge
    assert blocks == BLOCKS and (width // edge) & (width // edge - 1) == 0
    active = lax.broadcasted_iota(jnp.int32, (slots, targets), 0) < tile_count
    codes = jnp.where(active, tile_rows[0].T, blocks) * blocks + tile_cols[0].T
    head = load(((REACH, 1), (REACH - 1, 1), (REACH, 0)), tiles)

    def work(keep, give, partner=None, first=None, held=tiles, ahead=()):
        return tile_sums(keep, give, first, codes, columns, held, partner, ahead, tiles)

    (given,) = work(None, REACH, None, 0, head)
    partner = swap(given, "core")
    given, next_tiles = work(None, REACH - 1, None, SIDES, head, ((REACH - 1, 0),))
    late, near, cross = work(REACH, None, partner, SIDES + CORES * SIDES, head)
    message = late.reshape(-1, *late.shape[2:])
    partner = swap(given, "core")
    arrived = hop(message)
    crossed = swap(cross, "side")
    before = near
    late, near, cross = work(3, None, partner, 0, next_tiles)
    (given,) = work(None, 2)
    (message,) = sums(late, before, crossed, arrived, SIDES, 0)
    arrived_near = 1
    for step in (2, 3):
        distance = REACH - step
        partner = swap(given, "core")
        crossed = swap(cross, "side")
        arrived = hop(message)
        before = near
        late, near, cross, given = work(distance, distance - 1, partner)
        (message,) = sums(late, before, crossed, arrived, CORES * SIDES, arrived_near)
        arrived_near = CORES
    partner = swap(given, "core")
    crossed = swap(cross, "side")
    arrived = hop(message)
    before = near
    late, near, cross = work(0, None, partner)
    crossed_last = swap(cross, "side")
    message, moved = sums(None, before, crossed, arrived, CORES * SIDES, CORES, True)
    near_arrived = hop(message)
    moved = swap(moved, "core")
    late_cross = swap(across(late, arrived, moved), "side")
    near_moved = swap(second_half(near_arrived), "core")
    shares = degree.reshape(blocks, edge)
    operands = (near, crossed_last, near_arrived, near_moved, late, late_cross, arrived, moved, shares)
    neighbor = divide(groups, operands)
    gathered = lax.all_to_all(neighbor, "grp", split_axis=0, concat_axis=0)
    base = lax.dot_general(
        w_self, node_feats, (((0,), (0,)), ((), ())), preferred_element_type=jnp.float32
    )
    return finish(base, w_neigh, gathered)


def solution(mesh):
    fine = Mesh(
        mesh.devices.reshape(RINGS, SIDES, CORES, mesh.shape["grp"]), ("ring", "side", "core", "grp")
    )
    loop = ("ring", "side", "core")
    return jax.shard_map(
        shards,
        mesh=fine,
        in_specs=(
            P(None, (*loop, "grp")),
            P(loop, None, None, None, None),
            P(loop, None, None),
            P(loop, None, None),
            P(loop, None),
            P(loop),
            P(),
            P(),
        ),
        out_specs=P(None, (*loop, "grp")),
        check_vma=False,
    )
```

```python
import functools

import jax
import jax.numpy as jnp
from jax import lax
from jax.experimental import pallas as pl
from jax.experimental.pallas import tpu as pltpu
from jax.sharding import Mesh
from jax.sharding import PartitionSpec as P


RINGS = 8
SIDES = 2
CORES = 2
REACH = RINGS // 2
NEAR = 10
VMEM = 3 * 1024 * 1024
RESIDENT = pl.BlockSpec(memory_space=pltpu.VMEM)
SCALARS = pl.BlockSpec(memory_space=pltpu.SMEM)


def cores_at(distance):
    return 1 if distance in (0, REACH) else CORES


def small_call(body, operands, outs):
    return pl.pallas_call(
        body,
        in_specs=[RESIDENT] * len(operands),
        out_specs=[RESIDENT] * len(outs),
        out_shape=outs,
        compiler_params=pltpu.CompilerParams(vmem_limit_bytes=VMEM),
        cost_estimate=pl.CostEstimate(flops=500_000_000, bytes_accessed=1_000_000, transcendentals=0),
    )(*operands)


def target_of(distance, core_turn, side_turn, given):
    mine = lax.axis_index("core")
    by = jnp.where(mine == given, distance, RINGS - distance)
    ring = lax.rem(lax.axis_index("ring") + by, RINGS)
    side = lax.axis_index("side") ^ side_turn
    core = mine ^ given ^ core_turn
    return (ring * SIDES + side) * CORES + core


def add_tiles(total, target, codes, columns, tiles):
    slots, edge = tiles.shape[:2]
    blocks = total.shape[0]
    shift = blocks.bit_length() - 1
    per = columns.shape[2] // edge
    for slot in range(slots):
        code = codes[slot, target]
        row, col = code >> shift, code & (blocks - 1)
        lanes = pl.ds(pl.multiple_of((col & (per - 1)) * edge, edge), edge)
        chosen = columns[col >> (per.bit_length() - 1), :, lanes]
        chosen = jnp.where(row < blocks, chosen, jnp.zeros_like(chosen))
        total[row & (blocks - 1)] += lax.dot_general(
            chosen, tiles[slot], (((1,), (1,)), ((), ())), preferred_element_type=jnp.float32
        )


def copies_of(plan, source, out, done):
    copies = []
    for distance, given in plan:
        for core in range(cores_at(distance)):
            for side in range(SIDES):
                place = len(copies)
                target = target_of(distance, core, side, given)
                copies.append(pltpu.make_async_copy(source.at[target], out.at[place], done.at[place]))
    return copies


def places_of(plan):
    return sum(cores_at(distance) * SIDES for distance, _ in plan)


def tile_kernel(keep, give, first, ahead, codes, columns, tiles, *rest):
    copies = []
    if ahead:
        source, *rest, done = rest
        *rest, out, total = rest
        copies = copies_of(ahead, source, out, done)
    else:
        *rest, total = rest
    for copy in copies:
        copy.start()

    def add(distance, core, side, given):
        target = target_of(distance, core, side, given)
        place = target if first is None else first + core * SIDES + side
        add_tiles(total, target, codes, columns, tiles.at[place])

    if keep is not None:
        partner, late, near, cross = rest[:4]
        rest = rest[4:]

        @pl.loop(0, cores_at(keep))
        def _(core):
            for side in range(SIDES):
                index = core * SIDES + side
                total[...] = partner[index].astype(jnp.float32)
                add(keep, core, side, 0)
                late[index] = total[NEAR:].astype(late.dtype)
                out = near if side == 0 else cross
                out[core] = total[:NEAR].astype(out.dtype)

    if give is not None:
        given = rest[0]

        @pl.loop(0, cores_at(give))
        def _(core):
            for side in range(SIDES):
                total[...] = jnp.zeros_like(total)
                add(give, core, side, 1)
                given[core * SIDES + side] = total[...].astype(given.dtype)

    for copy in copies:
        copy.wait()


def tile_sums(keep, give, first, codes, columns, tiles, partner=None, ahead=(), source=None):
    edge = tiles.shape[2]
    groups, channels, width = columns.shape
    blocks = groups * width // edge
    outs = []
    work = 0
    if keep is not None:
        cores = cores_at(keep)
        work += cores * SIDES
        late = jnp.bfloat16 if keep == REACH else jnp.float32
        outs += [
            jax.ShapeDtypeStruct((cores * SIDES, blocks - NEAR, channels, edge), late),
            jax.ShapeDtypeStruct((cores, NEAR, channels, edge), jnp.float32),
            jax.ShapeDtypeStruct((cores, NEAR, channels, edge), jnp.bfloat16),
        ]
    if give is not None:
        cores = cores_at(give)
        work += cores * SIDES
        outs.append(jax.ShapeDtypeStruct((cores * SIDES, blocks, channels, edge), jnp.bfloat16))
    operands, specs = [columns, tiles], [RESIDENT, RESIDENT]
    scratch = [pltpu.VMEM((blocks, channels, edge), jnp.float32)]
    if ahead:
        operands.append(pltpu.with_memory_space_constraint(source, pltpu.HBM))
        specs.append(pl.BlockSpec(memory_space=pltpu.HBM))
        outs.append(jax.ShapeDtypeStruct((places_of(ahead), *source.shape[1:]), source.dtype))
        scratch.append(pltpu.SemaphoreType.DMA((places_of(ahead),)))
    if partner is not None:
        operands.append(partner)
        specs.append(RESIDENT)
    return pl.pallas_call(
        functools.partial(tile_kernel, keep, give, first, ahead),
        in_specs=[SCALARS] + specs,
        out_specs=[RESIDENT] * len(outs),
        out_shape=outs,
        scratch_shapes=scratch,
        compiler_params=pltpu.CompilerParams(vmem_limit_bytes=VMEM),
        cost_estimate=pl.CostEstimate(
            flops=work * 500_000_000, bytes_accessed=work * 800_000, transcendentals=0
        ),
    )(codes, *operands)


def load_kernel(plan, source, out, done):
    copies = copies_of(plan, source, out, done)
    for copy in copies:
        copy.start()
    for copy in copies:
        copy.wait()


def load(plan, tiles):
    count = places_of(plan)
    return pl.pallas_call(
        functools.partial(load_kernel, plan),
        in_specs=[pl.BlockSpec(memory_space=pltpu.HBM)],
        out_specs=RESIDENT,
        out_shape=jax.ShapeDtypeStruct((count, *tiles.shape[1:]), tiles.dtype),
        scratch_shapes=[pltpu.SemaphoreType.DMA((count,))],
        compiler_params=pltpu.CompilerParams(vmem_limit_bytes=256 * 1024),
        cost_estimate=pl.CostEstimate(flops=2_000_000_000, bytes_accessed=5_000_000, transcendentals=0),
    )(pltpu.with_memory_space_constraint(tiles, pltpu.HBM))


def late_kernel(here, arrived, send):
    for index in range(here.shape[0]):
        total = here[index]
        if index < arrived.shape[0]:
            total = total + arrived[index].astype(jnp.float32)
        send[index] = total.astype(send.dtype)


def pass_late(here, arrived):
    return small_call(late_kernel, (here, arrived), [jax.ShapeDtypeStruct(here.shape, jnp.bfloat16)])[0]


def near_kernel(here, crossed, *rest):
    *arrived, send = rest
    for core in range(here.shape[0]):
        total = here[core] + crossed[core].astype(jnp.float32)
        if arrived and core < arrived[0].shape[0]:
            total = total + arrived[0][core].astype(jnp.float32)
        send[core] = total.astype(send.dtype)


def pass_near(here, crossed, *arrived):
    out = jax.ShapeDtypeStruct(here.shape, jnp.bfloat16)
    return small_call(near_kernel, (here, crossed, *arrived), [out])[0]


def half_kernel(arrived, out):
    out[...] = arrived[pl.ds(out.shape[0], out.shape[0])]


def second_half(arrived):
    out = jax.ShapeDtypeStruct((arrived.shape[0] // 2, *arrived.shape[1:]), arrived.dtype)
    return small_call(half_kernel, (arrived,), [out])[0]


def across_kernel(here, arrived, moved, send):
    total = here[1] + arrived[1].astype(jnp.float32) + moved[1].astype(jnp.float32)
    send[...] = total.astype(send.dtype)


def across(here, arrived, moved):
    out = jax.ShapeDtypeStruct(here.shape[1:], jnp.bfloat16)
    return small_call(across_kernel, (here, arrived, moved), [out])[0]


def divide_kernel(near, near_cross, near_same, near_turned, late, late_cross, late_same, late_turned, degree, out):
    for block in range(degree.shape[0]):
        here, cross, same, turned, place = near, near_cross.at[0], near_same, near_turned, block
        if block >= NEAR:
            here, cross, same, turned, place = late, late_cross, late_same, late_turned, block - NEAR
        total = here[0, place] + cross[place].astype(jnp.float32)
        total = total + same[0, place].astype(jnp.float32) + turned[0, place].astype(jnp.float32)
        total = total / degree[block : block + 1].astype(jnp.float32)
        out[block // out.shape[1], block % out.shape[1]] = total.astype(out.dtype)


def divide(groups, operands):
    degree = operands[-1]
    blocks, edge = degree.shape
    out = jax.ShapeDtypeStruct((groups, blocks // groups, operands[0].shape[2], edge), jnp.bfloat16)
    return small_call(divide_kernel, operands, [out])[0]


def finish_kernel(base, weight, neighbors, out):
    edge = neighbors.shape[3]
    for part in range(neighbors.shape[1]):
        lanes = slice(part * edge, (part + 1) * edge)
        combined = base[:, lanes] + lax.dot_general(
            weight[...],
            neighbors[:, part].reshape(-1, edge),
            (((0,), (0,)), ((), ())),
            preferred_element_type=jnp.float32,
        )
        hidden = jnp.maximum(combined, 0.0)
        mean_square = jnp.mean(hidden * hidden, axis=0, keepdims=True)
        out[:, lanes] = (hidden * lax.rsqrt(mean_square + 1e-05)).astype(out.dtype)


def finish(base, weight, neighbors):
    return pl.pallas_call(
        finish_kernel,
        out_shape=jax.ShapeDtypeStruct(base.shape, jnp.bfloat16),
        compiler_params=pltpu.CompilerParams(vmem_limit_bytes=10 * 1024 * 1024),
    )(base, weight, neighbors)


def hop(values):
    pairs = []
    for ring in range(RINGS):
        for core in range(CORES):
            pairs.append((ring * CORES + core, (ring + 1 - 2 * core) % RINGS * CORES + core))
    return lax.ppermute(values, ("ring", "core"), pairs)


def swap(values, axis):
    return lax.ppermute(values, axis, [(0, 1), (1, 0)])


def shards(node_feats, tile_vals, tile_rows, tile_cols, tile_count, degree, w_self, w_neigh):
    groups = lax.axis_size("grp")
    features, width = node_feats.shape
    columns = lax.all_to_all(node_feats.reshape(groups, features // groups, width), "grp", split_axis=0, concat_axis=0)
    tiles = tile_vals[0]
    targets, slots, edge = tiles.shape[:3]
    blocks = groups * width // edge
    assert blocks & (blocks - 1) == 0 and (width // edge) & (width // edge - 1) == 0
    active = lax.broadcasted_iota(jnp.int32, (slots, targets), 0) < tile_count
    codes = jnp.where(active, tile_rows[0].T, blocks) * blocks + tile_cols[0].T
    head = load(((REACH, 1), (REACH - 1, 1), (REACH, 0)), tiles)

    def work(keep, give, partner=None, first=None, held=tiles, ahead=()):
        return tile_sums(keep, give, first, codes, columns, held, partner, ahead, tiles)

    (given,) = work(None, REACH, None, 0, head)
    partner = swap(given, "core")
    given, next_tiles = work(None, REACH - 1, None, SIDES, head, ((REACH - 1, 0),))
    late, near, cross = work(REACH, None, partner, SIDES + CORES * SIDES, head)
    message, near_back = late, ()
    for step in range(1, REACH + 1):
        distance = REACH - step
        partner = swap(given, "core")
        crossed = swap(cross, "side")
        arrived = hop(message)
        before = near
        if step == 1:
            (given,) = work(None, distance - 1)
            late, near, cross = work(distance, None, partner, 0, next_tiles)
        elif distance:
            late, near, cross, given = work(distance, distance - 1, partner)
        else:
            late, near, cross = work(distance, None, partner)
        if distance:
            message = pass_late(late, arrived)
        else:
            moved = swap(second_half(arrived), "core")
            late_cross = swap(across(late, arrived, moved), "side")
        near_message = pass_near(before, crossed, *near_back)
        near_back = (hop(near_message),)
    crossed = swap(cross, "side")
    near_moved = swap(second_half(*near_back), "core")
    shares = degree.reshape(blocks, edge)
    operands = (near, crossed, *near_back, near_moved, late, late_cross, arrived, moved, shares)
    neighbor = divide(groups, operands)
    gathered = lax.all_to_all(neighbor, "grp", split_axis=0, concat_axis=0)
    base = lax.dot_general(
        w_self, node_feats, (((0,), (0,)), ((), ())), preferred_element_type=jnp.float32
    )
    return finish(base, w_neigh, gathered)


def solution(mesh):
    fine = Mesh(
        mesh.devices.reshape(RINGS, SIDES, CORES, mesh.shape["grp"]), ("ring", "side", "core", "grp")
    )
    loop = ("ring", "side", "core")
    return jax.shard_map(
        shards,
        mesh=fine,
        in_specs=(
            P(None, (*loop, "grp")),
            P(loop, None, None, None, None),
            P(loop, None, None),
            P(loop, None, None),
            P(loop, None),
            P(loop),
            P(),
            P(),
        ),
        out_specs=P(None, (*loop, "grp")),
        check_vma=False,
    )
```

```python
import functools

import jax
import jax.numpy as jnp
from jax import lax
from jax.experimental import pallas as pl
from jax.experimental.pallas import tpu as pltpu
from jax.sharding import Mesh
from jax.sharding import PartitionSpec as P


RINGS = 8
SIDES = 2
CORES = 2
REACH = RINGS // 2
NEAR = 9
VMEM = 3 * 1024 * 1024
RESIDENT = pl.BlockSpec(memory_space=pltpu.VMEM)
SCALARS = pl.BlockSpec(memory_space=pltpu.SMEM)


def cores_at(distance):
    return 1 if distance in (0, REACH) else CORES


def small_call(body, operands, outs):
    return pl.pallas_call(
        body,
        in_specs=[RESIDENT] * len(operands),
        out_specs=[RESIDENT] * len(outs),
        out_shape=outs,
        compiler_params=pltpu.CompilerParams(vmem_limit_bytes=VMEM),
        cost_estimate=pl.CostEstimate(flops=500_000_000, bytes_accessed=1_000_000, transcendentals=0),
    )(*operands)


def target_of(distance, core_turn, side_turn, given):
    mine = lax.axis_index("core")
    by = jnp.where(mine == given, distance, RINGS - distance)
    ring = lax.rem(lax.axis_index("ring") + by, RINGS)
    side = lax.axis_index("side") ^ side_turn
    core = mine ^ given ^ core_turn
    return (ring * SIDES + side) * CORES + core


def add_tiles(total, target, codes, columns, tiles):
    slots, edge = tiles.shape[:2]
    blocks = total.shape[0]
    shift = blocks.bit_length() - 1
    per = columns.shape[2] // edge
    for slot in range(slots):
        code = codes[slot, target]
        row, col = code >> shift, code & (blocks - 1)
        lanes = pl.ds(pl.multiple_of((col & (per - 1)) * edge, edge), edge)
        chosen = columns[col >> (per.bit_length() - 1), :, lanes]
        chosen = jnp.where(row < blocks, chosen, jnp.zeros_like(chosen))
        total[row & (blocks - 1)] += lax.dot_general(
            chosen, tiles[slot], (((1,), (1,)), ((), ())), preferred_element_type=jnp.float32
        )


def copies_of(plan, source, out, done):
    copies = []
    for distance, given in plan:
        for core in range(cores_at(distance)):
            for side in range(SIDES):
                place = len(copies)
                target = target_of(distance, core, side, given)
                copies.append(pltpu.make_async_copy(source.at[target], out.at[place], done.at[place]))
    return copies


def places_of(plan):
    return sum(cores_at(distance) * SIDES for distance, _ in plan)


def tile_kernel(keep, give, first, ahead, offset, codes, columns, tiles, *rest):
    copies = []
    if ahead:
        source, *rest, done = rest
        *rest, out, even, odd = rest
        copies = copies_of(ahead, source, out, done)
    else:
        *rest, even, odd = rest
    for copy in copies:
        copy.start()

    def add(total, distance, core, side, given):
        target = target_of(distance, core, side, given)
        place = target if first is None else first + core * SIDES + side
        add_tiles(total, target, codes, columns, tiles.at[place])

    if keep is not None:
        partner, rest = rest[0], rest[1:]
        for core in range(cores_at(keep)):
            for side in range(SIDES):
                index = core * SIDES + side
                total = odd if side else even
                total[...] = partner[offset + index].astype(jnp.float32)
                add(total, keep, core, side, 0)
                if keep == REACH:
                    rest[0][index] = total[...].astype(rest[0].dtype)
                else:
                    late, near, cross = rest[:3]
                    late[index] = total[NEAR:].astype(late.dtype)
                    out = near if side == 0 else cross
                    out[core] = total[:NEAR].astype(out.dtype)
        rest = rest[1:] if keep == REACH else rest[3:]

    place = 0
    for distance in give:
        for core in range(cores_at(distance)):
            for side in range(SIDES):
                total = odd if side else even
                total[...] = jnp.zeros_like(total)
                add(total, distance, core, side, 1)
                rest[0][place] = total[...].astype(rest[0].dtype)
                place += 1

    for copy in copies:
        copy.wait()


def tile_sums(keep, give, first, codes, columns, tiles, partner=None, ahead=(), source=None, offset=0):
    edge = tiles.shape[2]
    groups, channels, width = columns.shape
    blocks = groups * width // edge
    outs = []
    work = 0
    if keep is not None:
        cores = cores_at(keep)
        work += cores * SIDES
        if keep == REACH:
            outs.append(jax.ShapeDtypeStruct((cores * SIDES, blocks, channels, edge), jnp.bfloat16))
        else:
            crossing = jnp.float32 if keep == REACH - 1 else jnp.bfloat16
            outs += [
                jax.ShapeDtypeStruct((cores * SIDES, blocks - NEAR, channels, edge), jnp.float32),
                jax.ShapeDtypeStruct((cores, NEAR, channels, edge), jnp.float32),
                jax.ShapeDtypeStruct((cores, NEAR, channels, edge), crossing),
            ]
    if give:
        count = sum(cores_at(distance) * SIDES for distance in give)
        work += count
        outs.append(jax.ShapeDtypeStruct((count, blocks, channels, edge), jnp.bfloat16))
    operands, specs = [columns, tiles], [RESIDENT, RESIDENT]
    scratch = [pltpu.VMEM((blocks, channels, edge), jnp.float32)] * 2
    if ahead:
        operands.append(pltpu.with_memory_space_constraint(source, pltpu.HBM))
        specs.append(pl.BlockSpec(memory_space=pltpu.HBM))
        outs.append(jax.ShapeDtypeStruct((places_of(ahead), *source.shape[1:]), source.dtype))
        scratch.append(pltpu.SemaphoreType.DMA((places_of(ahead),)))
    if partner is not None:
        operands.append(partner)
        specs.append(RESIDENT)
    return pl.pallas_call(
        functools.partial(tile_kernel, keep, give, first, ahead, offset),
        in_specs=[SCALARS] + specs,
        out_specs=[RESIDENT] * len(outs),
        out_shape=outs,
        scratch_shapes=scratch,
        compiler_params=pltpu.CompilerParams(vmem_limit_bytes=VMEM),
        cost_estimate=pl.CostEstimate(
            flops=work * 500_000_000, bytes_accessed=work * 800_000, transcendentals=0
        ),
    )(codes, *operands)


def load_kernel(plan, source, out, done):
    copies = copies_of(plan, source, out, done)
    for copy in copies:
        copy.start()
    for copy in copies:
        copy.wait()


def load(plan, tiles):
    count = places_of(plan)
    return pl.pallas_call(
        functools.partial(load_kernel, plan),
        in_specs=[pl.BlockSpec(memory_space=pltpu.HBM)],
        out_specs=RESIDENT,
        out_shape=jax.ShapeDtypeStruct((count, *tiles.shape[1:]), tiles.dtype),
        scratch_shapes=[pltpu.SemaphoreType.DMA((count,))],
        compiler_params=pltpu.CompilerParams(vmem_limit_bytes=256 * 1024),
        cost_estimate=pl.CostEstimate(flops=2_000_000_000, bytes_accessed=5_000_000, transcendentals=0),
    )(pltpu.with_memory_space_constraint(tiles, pltpu.HBM))


def first_kernel(late, near, cross, arrived, send, base, crossing):
    for index in range(late.shape[0]):
        total = late[index]
        if index < arrived.shape[0]:
            total = total + arrived[index, pl.ds(NEAR, total.shape[0])].astype(jnp.float32)
        send[index] = total.astype(send.dtype)
    for core in range(near.shape[0]):
        mine, other = near[core], cross[core]
        if core == 0:
            mine = mine + arrived[0, pl.ds(0, NEAR)].astype(jnp.float32)
            other = other + arrived[1, pl.ds(0, NEAR)].astype(jnp.float32)
        base[core] = mine
        crossing[core] = other.astype(crossing.dtype)


def pass_first(late, near, cross, arrived):
    outs = [
        jax.ShapeDtypeStruct(late.shape, jnp.bfloat16),
        jax.ShapeDtypeStruct(near.shape, jnp.float32),
        jax.ShapeDtypeStruct(near.shape, jnp.bfloat16),
    ]
    return small_call(first_kernel, (late, near, cross, arrived), outs)


def late_kernel(here, arrived, send):
    for index in range(here.shape[0]):
        total = here[index]
        if index < arrived.shape[0]:
            total = total + arrived[index].astype(jnp.float32)
        send[index] = total.astype(send.dtype)


def pass_late(here, arrived):
    return small_call(late_kernel, (here, arrived), [jax.ShapeDtypeStruct(here.shape, jnp.bfloat16)])[0]


def near_kernel(here, crossed, *rest):
    *arrived, send = rest
    for core in range(here.shape[0]):
        total = here[core] + crossed[core].astype(jnp.float32)
        if arrived and core < arrived[0].shape[0]:
            total = total + arrived[0][core].astype(jnp.float32)
        send[core] = total.astype(send.dtype)


def pass_near(here, crossed, *arrived):
    out = jax.ShapeDtypeStruct(here.shape, jnp.bfloat16)
    return small_call(near_kernel, (here, crossed, *arrived), [out])[0]


def half_kernel(arrived, out):
    out[...] = arrived[pl.ds(out.shape[0], out.shape[0])]


def second_half(arrived):
    out = jax.ShapeDtypeStruct((arrived.shape[0] // 2, *arrived.shape[1:]), arrived.dtype)
    return small_call(half_kernel, (arrived,), [out])[0]


def across_kernel(here, arrived, moved, send):
    total = here[1] + arrived[1].astype(jnp.float32) + moved[1].astype(jnp.float32)
    send[...] = total.astype(send.dtype)


def across(here, arrived, moved):
    out = jax.ShapeDtypeStruct(here.shape[1:], jnp.bfloat16)
    return small_call(across_kernel, (here, arrived, moved), [out])[0]


def divide_kernel(near, near_cross, near_same, near_turned, late, late_cross, late_same, late_turned, degree, out):
    for block in range(degree.shape[0]):
        here, cross, same, turned, place = near, near_cross.at[0], near_same, near_turned, block
        if block >= NEAR:
            here, cross, same, turned, place = late, late_cross, late_same, late_turned, block - NEAR
        total = here[0, place] + cross[place].astype(jnp.float32)
        total = total + same[0, place].astype(jnp.float32) + turned[0, place].astype(jnp.float32)
        total = total / degree[block : block + 1].astype(jnp.float32)
        out[block // out.shape[1], block % out.shape[1]] = total.astype(out.dtype)


def divide(groups, operands):
    degree = operands[-1]
    blocks, edge = degree.shape
    out = jax.ShapeDtypeStruct((groups, blocks // groups, operands[0].shape[2], edge), jnp.bfloat16)
    return small_call(divide_kernel, operands, [out])[0]


def finish_kernel(base, weight, neighbors, out):
    edge = neighbors.shape[3]
    for part in range(neighbors.shape[1]):
        lanes = slice(part * edge, (part + 1) * edge)
        combined = base[:, lanes] + lax.dot_general(
            weight[...],
            neighbors[:, part].reshape(-1, edge),
            (((0,), (0,)), ((), ())),
            preferred_element_type=jnp.float32,
        )
        hidden = jnp.maximum(combined, 0.0)
        mean_square = jnp.mean(hidden * hidden, axis=0, keepdims=True)
        out[:, lanes] = (hidden * lax.rsqrt(mean_square + 1e-05)).astype(out.dtype)


def finish(base, weight, neighbors):
    return pl.pallas_call(
        finish_kernel,
        out_shape=jax.ShapeDtypeStruct(base.shape, jnp.bfloat16),
        compiler_params=pltpu.CompilerParams(vmem_limit_bytes=10 * 1024 * 1024),
    )(base, weight, neighbors)


def hop(values):
    pairs = []
    for ring in range(RINGS):
        for core in range(CORES):
            pairs.append((ring * CORES + core, (ring + 1 - 2 * core) % RINGS * CORES + core))
    return lax.ppermute(values, ("ring", "core"), pairs)


def swap(values, axis):
    return lax.ppermute(values, axis, [(0, 1), (1, 0)])


def shards(node_feats, tile_vals, tile_rows, tile_cols, tile_count, degree, w_self, w_neigh):
    groups = lax.axis_size("grp")
    features, width = node_feats.shape
    columns = lax.all_to_all(node_feats.reshape(groups, features // groups, width), "grp", split_axis=0, concat_axis=0)
    tiles = tile_vals[0]
    targets, slots, edge = tiles.shape[:3]
    blocks = groups * width // edge
    assert blocks & (blocks - 1) == 0 and (width // edge) & (width // edge - 1) == 0
    active = lax.broadcasted_iota(jnp.int32, (slots, targets), 0) < tile_count
    codes = jnp.where(active, tile_rows[0].T, blocks) * blocks + tile_cols[0].T
    head = load(((REACH, 1), (REACH - 1, 1), (REACH, 0)), tiles)

    def work(keep, give, partner=None, first=None, held=tiles, ahead=(), offset=0):
        return tile_sums(keep, give, first, codes, columns, held, partner, ahead, tiles, offset)

    (given,) = work(None, (REACH,), None, 0, head)
    partner = swap(given, "core")
    given, next_tiles = work(None, (REACH - 1,), None, SIDES, head, ((REACH - 1, 0),))
    (message,) = work(REACH, (), partner, SIDES + CORES * SIDES, head)
    partner = swap(given, "core")
    arrived = hop(message)
    (given,) = work(None, tuple(range(REACH - 2, -1, -1)))
    late, near, cross = work(REACH - 1, (), partner, 0, next_tiles)
    partner = swap(given, "core")
    message, near, cross = pass_first(late, near, cross, arrived)
    near_back = ()
    for step in range(2, REACH + 1):
        distance = REACH - step
        crossed = swap(cross, "side")
        arrived = hop(message)
        before = near
        offset = (step - 2) * CORES * SIDES
        late, near, cross = work(distance, (), partner, offset=offset)
        if distance:
            message = pass_late(late, arrived)
        else:
            moved = swap(second_half(arrived), "core")
            late_cross = swap(across(late, arrived, moved), "side")
        near_message = pass_near(before, crossed, *near_back)
        near_back = (hop(near_message),)
    crossed = swap(cross, "side")
    near_moved = swap(second_half(*near_back), "core")
    shares = degree.reshape(blocks, edge)
    operands = (near, crossed, *near_back, near_moved, late, late_cross, arrived, moved, shares)
    neighbor = divide(groups, operands)
    gathered = lax.all_to_all(neighbor, "grp", split_axis=0, concat_axis=0)
    base = lax.dot_general(
        w_self, node_feats, (((0,), (0,)), ((), ())), preferred_element_type=jnp.float32
    )
    return finish(base, w_neigh, gathered)


def solution(mesh):
    fine = Mesh(
        mesh.devices.reshape(RINGS, SIDES, CORES, mesh.shape["grp"]), ("ring", "side", "core", "grp")
    )
    loop = ("ring", "side", "core")
    return jax.shard_map(
        shards,
        mesh=fine,
        in_specs=(
            P(None, (*loop, "grp")),
            P(loop, None, None, None, None),
            P(loop, None, None),
            P(loop, None, None),
            P(loop, None),
            P(loop),
            P(),
            P(),
        ),
        out_specs=P(None, (*loop, "grp")),
        check_vma=False,
    )
```
